32 devices in a mesh: ctx: 4 (over y, core), fsdp: 8 (over z, x).
Axes of the slice: x: 2, y: 2, z: 4, core: 2. Of those that a mesh axis runs over, the one named last changes fastest.
Arguments:
- tokens: bfloat16 [8, 1024, 768], P('fsdp', 'ctx')
- cotangent: bfloat16 [8, 1024, 768], P('fsdp', 'ctx'), may hold values from -6 to 6
- lengths: int32 [8], P('fsdp'), may hold values from 512 to 1024, as said below
- w_query: float32 [768, 768], P('fsdp'), may hold values from -0.5 to 0.5
- w_key: float32 [768, 768], P('fsdp'), may hold values from -0.5 to 0.5
- w_value: float32 [768, 768], P('fsdp'), may hold values from -0.21875 to 0.21875
- w_out: float32 [768, 768], P('fsdp'), may hold values from -0.21875 to 0.21875
- w_up: float32 [768, 3072], P('fsdp'), may hold values from -0.21875 to 0.21875
- w_down: float32 [3072, 768], P('fsdp'), may hold values from -0.109375 to 0.109375
- b_query: float32 [768], P('fsdp'), may hold values from -6 to 6
- b_value: float32 [768], P('fsdp'), may hold values from -1.75 to 1.75
- b_out: float32 [768], P('fsdp'), may hold values from -1.75 to 1.75
- b_up: float32 [3072], P('fsdp'), may hold values from -1.75 to 1.75
- b_down: float32 [768], P('fsdp'), may hold values from -1.75 to 1.75
- gain_first: float32 [768], P('fsdp'), may hold values from 0.25 to 1.75
- shift_first: float32 [768], P('fsdp'), may hold values from -1.75 to 1.75
- gain_second: float32 [768], P('fsdp'), may hold values from 0.25 to 1.75
- shift_second: float32 [768], P('fsdp'), may hold values from -1.75 to 1.75
- conv_taps: float32 [12, 33], replicated, may hold values from -1 to 1
Outputs:
- output: bfloat16 [8, 1024, 768], P('fsdp', 'ctx')
- input_grad: bfloat16 [8, 1024, 768], P('fsdp', 'ctx')
- grad_w_query: float32 [768, 768], P('fsdp')
- grad_w_key: float32 [768, 768], P('fsdp')
- grad_w_value: float32 [768, 768], P('fsdp')
- grad_w_out: float32 [768, 768], P('fsdp')
- grad_w_up: float32 [768, 3072], P('fsdp')
- grad_w_down: float32 [3072, 768], P('fsdp')
- grad_b_query: float32 [768], P('fsdp')
- grad_b_value: float32 [768], P('fsdp')
- grad_b_out: float32 [768], P('fsdp')
- grad_b_up: float32 [3072], P('fsdp')
- grad_b_down: float32 [768], P('fsdp')
- grad_gain_first: float32 [768], P('fsdp')
- grad_shift_first: float32 [768], P('fsdp')
- grad_gain_second: float32 [768], P('fsdp')
- grad_shift_second: float32 [768], P('fsdp')
- grad_conv_taps: float32 [12, 33], replicated
The draws below stay inside these ranges and needn't reach their ends.
Inputs may be any that keep to these rules, and one draw needn't show every extreme that they name: The first lengths[s] slots of sequence s are valid, the rest padding; some sequence fills all 1024 slots.
All inputs are finite; a program needn't handle non-finite values.
Results may differ from the reference program's by a relative error of at most 0.025.
The reference program's roundings to bfloat16 on the way count: a program that leaves them out, or rounds other values in their place, can miss the bound.
Values may be sent and summed in bfloat16 or wider, within the bound.
No kernel may reach another device: no remote copies, remote signals or barrier semaphores. Data moves between devices by JAX's collectives and lax.ppermute only.
A program may use at most 192 MiB of HBM per device.

```python
import jax
import jax.numpy as jnp
from jax import lax

D = 768
HEADS = 12
HEAD_DIM = 64
FF = 3072
LAND = 64
KSIZE = 33
ITERS = 6
SLOT = 1024
SEQS = 8
HALF = 16


def draw_tokens(key, part):
    rough = jax.random.normal(jax.random.fold_in(key, 11), (SEQS, SLOT, D), jnp.float32)
    blocks = jax.random.normal(jax.random.fold_in(key, 12), (SEQS, SLOT // 32, D), jnp.float32)
    return (0.6 * rough + 0.8 * jnp.repeat(blocks, 32, axis=1)).astype(jnp.bfloat16)


def draw_lengths(key, part):
    drawn = jax.random.randint(jax.random.fold_in(key, 21), (SEQS,), SLOT // 2, SLOT + 1, dtype=jnp.int32)
    full_at = jax.random.randint(jax.random.fold_in(key, 22), (), 0, SEQS, dtype=jnp.int32)
    return jnp.where(jnp.arange(SEQS, dtype=jnp.int32) == full_at, SLOT, drawn).astype(jnp.int32)


def shard_levels(stream_key, dims, pieces, smallest, high):
    gain, own = 1.0, jax.random.fold_in(stream_key, 6)
    for dim, parts in pieces:
        heights = jnp.exp(jax.random.uniform(jax.random.fold_in(own, dim), (parts,), jnp.float32, smallest / len(pieces), high / len(pieces)))
        gain = gain * jnp.repeat(heights, dims[dim] // parts).reshape([-1 if axis == dim else 1 for axis in range(len(dims))])
    return gain


def normal_values(stream_key, extent, width, most, split=(), kind=jnp.bfloat16):
    values = width * jax.random.normal(stream_key, extent, jnp.float32)
    if split:
        values = values * shard_levels(stream_key, extent, split, -0.22, 0.18)
    return jnp.clip(values, -most, most).astype(kind)


def setup_inputs(seed: int = 0) -> dict:
    key_of = jax.random.split(jax.random.key(seed), 20)
    return {
        "tokens": draw_tokens(jax.random.fold_in(key_of[19], 71), 0),
        "cotangent": normal_values(key_of[1], (SEQS, SLOT, D), 1.0, 6.0, ((0, 8), (1, 4))),
        "lengths": draw_lengths(jax.random.fold_in(key_of[19], 71), 0),
        "w_query": normal_values(key_of[3], (D, D), (D // 5) ** -0.5, 0.5, ((0, 8),), jnp.float32),
        "w_key": normal_values(key_of[4], (D, D), (D // 5) ** -0.5, 0.5, ((0, 8),), jnp.float32),
        "w_value": normal_values(key_of[5], (D, D), D ** -0.5, 0.21875, ((0, 8),), jnp.float32),
        "w_out": normal_values(key_of[6], (D, D), D ** -0.5, 0.21875, ((0, 8),), jnp.float32),
        "w_up": normal_values(key_of[7], (D, FF), D ** -0.5, 0.21875, ((0, 8),), jnp.float32),
        "w_down": normal_values(key_of[8], (FF, D), FF ** -0.5, 0.109375, ((0, 8),), jnp.float32),
        "b_query": normal_values(key_of[9], (D,), 1.0, 6.0, ((0, 8),), jnp.float32),
        "b_value": normal_values(key_of[10], (D,), 0.3, 1.75, ((0, 8),), jnp.float32),
        "b_out": normal_values(key_of[11], (D,), 0.3, 1.75, ((0, 8),), jnp.float32),
        "b_up": normal_values(key_of[12], (FF,), 0.3, 1.75, ((0, 8),), jnp.float32),
        "b_down": normal_values(key_of[13], (D,), 0.3, 1.75, ((0, 8),), jnp.float32),
        "gain_first": jnp.clip(1.0 + 0.15 * jax.random.normal(key_of[14], (D,), jnp.float32), 0.25, 1.75),
        "shift_first": normal_values(key_of[15], (D,), 0.3, 1.75, ((0, 8),), jnp.float32),
        "gain_second": jnp.clip(1.0 + 0.15 * jax.random.normal(key_of[16], (D,), jnp.float32), 0.25, 1.75),
        "shift_second": normal_values(key_of[17], (D,), 0.3, 1.75, ((0, 8),), jnp.float32),
        "conv_taps": normal_values(key_of[18], (HEADS, KSIZE), 0.17, 1.0, (), jnp.float32),
    }


@jax.custom_vjp
def low(v):
    return lax.optimization_barrier(v.astype(jnp.bfloat16)).astype(jnp.float32)

@jax.custom_vjp
def low_back(v):
    return v

def low_keep(v):
    return (low(v), None)

def low_pass(kept, grad):
    return (grad,)

def back_keep(v):
    return (v, None)

def back_low(kept, grad):
    return (low(grad),)
low.defvjp(low_keep, low_pass)
low_back.defvjp(back_keep, back_low)
highest = lax.Precision.HIGHEST
norm_eps = 1e-05
masked_score = -1e+30

def matmul(left, right):
    return jnp.dot(left, right, precision=highest)

def layer_norm(features, weight_gain, weight_shift):
    average = lax.optimization_barrier(jnp.mean(features, axis=-1, keepdims=True))
    centered = features - average
    spread = lax.optimization_barrier(jnp.mean(centered * centered, axis=-1, keepdims=True))
    return centered * lax.rsqrt(spread + norm_eps) * weight_gain + weight_shift

def newton_inverse(kernel):
    column_top = lax.optimization_barrier(jnp.max(lax.optimization_barrier(jnp.sum(kernel, axis=1)), axis=-1))
    row_top = lax.optimization_barrier(jnp.max(lax.optimization_barrier(jnp.sum(kernel, axis=2)), axis=-1))
    approx = jnp.swapaxes(kernel, 1, 2) / (column_top * row_top)[:, None, None]
    identity = jnp.eye(kernel.shape[1], dtype=kernel.dtype)
    for iteration in range(ITERS):
        product = jnp.einsum('hij,hjk->hik', kernel, approx, precision=highest)
        factor = 7.0 * identity - product
        factor = 15.0 * identity - jnp.einsum('hij,hjk->hik', product, factor, precision=highest)
        factor = 13.0 * identity - jnp.einsum('hij,hjk->hik', product, factor, precision=highest)
        approx = 0.25 * jnp.einsum('hij,hjk->hik', approx, factor, precision=highest)
    return approx

def landmark_inverse(land_query, land_keys):
    query_heads = land_query.reshape(LAND, HEADS, HEAD_DIM)
    key_heads = land_keys.reshape(LAND, HEADS, HEAD_DIM)
    scores = jnp.einsum('ihe,jhe->hij', query_heads, key_heads, precision=highest)
    return newton_inverse(jax.nn.softmax(scores, axis=-1))

def conv_apply(padded, taps, count):
    padded_heads = padded.reshape(padded.shape[0], HEADS, HEAD_DIM)
    summed = jnp.zeros((count, HEADS, HEAD_DIM), jnp.float32)
    for offset in range(KSIZE):
        summed = summed + taps[:, offset][None, :, None] * padded_heads[offset:offset + count]
    return summed

def layer(inputs, parameters, taps, seg_table, counts, mask_col, is_valid):
    w_query, w_key, w_value, w_out, w_up, w_down, b_query, b_value, b_out, b_up, b_down, gain_first, shift_first, gain_second, shift_second = tuple((low(item) for item in parameters))
    slot_count = inputs.shape[0]
    queries = low(low_back((matmul(inputs, w_query) + b_query) * mask_col * 0.125))
    keys_low = low(low_back(matmul(inputs, w_key) * mask_col))
    values = low(low_back((matmul(inputs, w_value) + b_value) * mask_col))
    land_query = matmul(seg_table, queries) / counts[:, None]
    land_keys = matmul(seg_table, keys_low) / counts[:, None]
    query_heads = queries.reshape(slot_count, HEADS, HEAD_DIM)
    key_heads = keys_low.reshape(slot_count, HEADS, HEAD_DIM)
    value_heads = values.reshape(slot_count, HEADS, HEAD_DIM)
    land_keys_low = low(land_keys).reshape(LAND, HEADS, HEAD_DIM)
    land_query_low = low(land_query).reshape(LAND, HEADS, HEAD_DIM)
    scores_one = low_back(jnp.einsum('the,jhe->htj', query_heads, land_keys_low, precision=highest))
    kernel_one = low(jax.nn.softmax(scores_one, axis=-1))
    inverse = landmark_inverse(land_query, land_keys)
    scores_three = low_back(jnp.einsum('ihe,the->hit', land_query_low, key_heads, precision=highest))
    scores_three = jnp.where(is_valid[None, None, :], scores_three, masked_score)
    kernel_three = low(jax.nn.softmax(scores_three, axis=-1))
    context = low_back(jnp.einsum('hit,the->hie', kernel_three, value_heads, precision=highest))
    mixing = low(jnp.einsum('hij,hje->hie', inverse, context, precision=highest))
    attention = jnp.einsum('htj,hje->the', kernel_one, mixing, precision=highest)
    padded = jnp.pad(values, ((HALF, HALF), (0, 0)))
    conv_out = conv_apply(padded, taps, slot_count)
    mixed = low(low_back((attention + conv_out).reshape(slot_count, D)))
    mixer_out = low_back(matmul(mixed, w_out) + b_out)
    hidden = layer_norm(inputs + mixer_out, gain_first, shift_first)
    lifted = low_back(matmul(low(hidden), w_up) + b_up)
    active = low(jax.nn.gelu(lifted, approximate=False))
    feed_out = low_back(matmul(active, w_down) + b_down)
    return layer_norm(hidden + feed_out, gain_second, shift_second) * mask_col

def reference(tokens, cotangent, lengths, w_query, w_key, w_value, w_out, w_up, w_down, b_query, b_value, b_out, b_up, b_down, gain_first, shift_first, gain_second, shift_second, conv_taps):
    masters = (w_query, w_key, w_value, w_out, w_up, w_down, b_query, b_value, b_out, b_up, b_down, gain_first, shift_first, gain_second, shift_second)

    def one_sequence(totals, sequence_items):
        rows_in, grads_in, length = sequence_items
        inputs = rows_in.astype(jnp.float32)
        position = jnp.arange(SLOT, dtype=jnp.int32)
        is_valid = position < length
        landmark_ids = jnp.arange(LAND, dtype=jnp.int32)
        seg_table = ((position[None, :] * LAND // length == landmark_ids[:, None]) & is_valid[None, :]).astype(jnp.float32)
        counts = lax.optimization_barrier(jnp.sum(seg_table, axis=1))
        mask_col = is_valid.astype(jnp.float32)[:, None]

        def forward(layer_in, parameters, taps):
            return layer(layer_in, parameters, taps, seg_table, counts, mask_col, is_valid)
        result, pullback = jax.vjp(forward, inputs, masters, conv_taps)
        d_inputs, d_params, d_taps = pullback(grads_in.astype(jnp.float32))
        totals = jax.tree.map(jnp.add, totals, (d_params, d_taps))
        return (totals, (result.astype(jnp.bfloat16), d_inputs.astype(jnp.bfloat16)))
    zeros = jax.tree.map(jnp.zeros_like, (masters, conv_taps))
    (d_params, d_taps), (outputs, d_inputs) = lax.scan(one_sequence, zeros, (tokens, cotangent, lengths))
    return (outputs, d_inputs, d_params[0], d_params[1], d_params[2], d_params[3], d_params[4], d_params[5], d_params[6], d_params[7], d_params[8], d_params[9], d_params[10], d_params[11], d_params[12], d_params[13], d_params[14], d_taps)
```

```python
import jax
import jax.numpy as jnp
from jax import lax
from jax.experimental import pallas as pl
from jax.experimental.pallas import tpu as pltpu
from jax.sharding import PartitionSpec as P

D = 768
HEADS = 12
HEAD_DIM = 64
FF = 3072
LAND = 64
KSIZE = 33
ITERS = 6
HALF = 16

F32 = jnp.float32
BF = jnp.bfloat16
highest = lax.Precision.HIGHEST
norm_eps = 1e-05
masked_score = -1e30
CONV_OUT = 256
CONV_IN = 512
TAPS_OUT = 128
TAPS_IN = 384


def nn(a, b, **kw):
    return lax.dot_general(a, b, (((1,), (0,)), ((), ())), preferred_element_type=F32, **kw)


def nt(a, b, **kw):
    return lax.dot_general(a, b, (((1,), (1,)), ((), ())), preferred_element_type=F32, **kw)


def tn(a, b, **kw):
    return lax.dot_general(a, b, (((0,), (0,)), ((), ())), preferred_element_type=F32, **kw)


def shape(dims, dtype):
    return jax.ShapeDtypeStruct(dims, dtype)


SMEM = pl.BlockSpec(memory_space=pltpu.SMEM)
VMEM = pl.BlockSpec(memory_space=pltpu.VMEM)
ANY = pl.BlockSpec(memory_space=pl.ANY)


def swap(block, axis, key):
    count = lax.axis_size(axis)
    return lax.ppermute(block, axis, [(i, i ^ key) for i in range(count)])


def iota(dims, axis):
    return lax.broadcasted_iota(jnp.int32, dims, axis)


def fetch(copies):
    for copy in copies:
        copy.start()
    for copy in copies:
        copy.wait()


def halves(value):
    high = value.astype(BF)
    low = (value - high.astype(F32)).astype(BF)
    return high, low


def taps_kernel(base_ref, ahead_ref, back_ref):
    heads = base_ref.shape[0]
    for head in range(heads):
        for row, out_ref in ((0, ahead_ref), (1, back_ref)):
            line = jnp.broadcast_to(base_ref[head, row : row + 1, :], (CONV_IN, CONV_IN))
            band = pltpu.roll(line, 0, 1, stride=1, stride_axis=0)[:, :CONV_OUT]
            high, low = halves(band)
            out_ref[head, 0] = high
            out_ref[head, 1] = low


def taps_bands(taps):
    heads = taps.shape[0]
    ahead = jnp.pad(taps[:, ::-1], ((0, 0), (CONV_IN - 144, 144 - KSIZE)))
    back = jnp.pad(taps, ((0, 0), (CONV_IN - 144, 144 - KSIZE)))
    base = jnp.stack([ahead, back], axis=1)
    base = jnp.pad(base, ((0, 0), (0, 6), (0, 0)))
    band = shape((heads, 2, CONV_IN, CONV_OUT), BF)
    return pl.pallas_call(taps_kernel, out_shape=(band, band), name="bands")(base)


def conv_band(line, band_ref, head):
    slots = line.shape[1]
    blocks = slots // CONV_OUT
    edge = jnp.zeros((line.shape[0], 128), line.dtype)
    padded = jnp.concatenate([edge, line, edge], axis=1)
    stacked = jnp.concatenate(
        [padded[:, CONV_OUT * b : CONV_OUT * b + CONV_IN] for b in range(blocks)], axis=0
    )
    product = nn(stacked, band_ref[head, 0]) + nn(stacked, band_ref[head, 1])
    rows = line.shape[0]
    return jnp.concatenate([product[rows * b : rows * (b + 1)] for b in range(blocks)], axis=1)


def softmax_rows(scores):
    top = jnp.max(scores, axis=1, keepdims=True)
    powers = jnp.exp(scores - top)
    return powers / jnp.sum(powers, axis=1, keepdims=True)


def softmax_columns(scores):
    top = jnp.max(scores, axis=0, keepdims=True)
    powers = jnp.exp(scores - top)
    return powers / jnp.sum(powers, axis=0, keepdims=True)


def segments(slots, length):
    spot = iota((LAND, slots), 1)
    scaled = spot * LAND
    mark = iota((LAND, slots), 0) * length
    inside = (scaled >= mark) & (scaled < mark + length) & (spot < length)
    return jnp.where(inside, 1.0, 0.0)


def attend_kernel(parts, count_ctx, count_fsdp, *refs):
    heads, rows, shard = parts
    width = heads * HEAD_DIM
    refs = list(refs)
    scalar_ref = refs.pop(0)
    token_refs = [refs.pop(0) for _ in range(count_ctx)]
    weight_refs = [refs.pop(0) for _ in range(count_fsdp)]
    band_ref = refs.pop(0)
    (
        seq_ref,
        turned_ref,
        qkv_ref,
        small_ref,
        land_ref,
        state_ref,
        blocks_ref,
        joined_ref,
        extra_ref,
        mixed_ref,
        copy_sem,
    ) = refs
    own_ctx = scalar_ref[0]
    own_fsdp = scalar_ref[1]
    length = scalar_ref[2]
    slots = rows * count_ctx
    copies = []
    for key in range(count_ctx):
        spot = pl.multiple_of(jnp.bitwise_xor(own_ctx, key) * rows, rows)
        copies.append(
            pltpu.make_async_copy(
                token_refs[key], seq_ref.at[pl.ds(spot, rows), :], copy_sem.at[len(copies)]
            )
        )
    for key in range(count_fsdp):
        owner = jnp.bitwise_xor(own_fsdp, key)
        spot = pl.multiple_of(owner * shard, 8)
        copies.append(
            pltpu.make_async_copy(
                weight_refs[key].at[pl.ds(0, shard), :],
                joined_ref.at[pl.ds(spot, shard), :],
                copy_sem.at[len(copies)],
            )
        )
        spot = pl.multiple_of(owner * 8, 8)
        copies.append(
            pltpu.make_async_copy(
                weight_refs[key].at[pl.ds(shard, 8), :],
                extra_ref.at[pl.ds(spot, 8), :],
                copy_sem.at[len(copies)],
            )
        )
    fetch(copies)
    small_ref[...] = extra_ref[...]
    turned_ref[...] = joined_ref[...].T

    entry = iota((3 * width, 1), 0)
    kind = jnp.where(entry >= 2 * width, 2, jnp.where(entry >= width, 1, 0))
    spot = own_ctx * width + entry - kind * width
    owner = jnp.floor((spot.astype(F32) + 0.5) * (1.0 / shard)).astype(jnp.int32)
    lane = spot - owner * shard
    source = owner * 8 + jnp.where(kind == 2, 1, 0)
    wanted = (kind != 1) & (spot < D)
    choice = (iota((3 * width, count_fsdp * 8), 1) == source) & wanted
    spread = nn(choice.astype(BF), extra_ref[:, :128])
    bias = jnp.sum(
        jnp.where(iota((3 * width, 128), 1) == lane, spread, 0.0), axis=1, keepdims=True
    )
    scale = jnp.where(kind == 0, 0.125, 1.0)

    for chunk in range(slots // 256):
        begin = chunk * 256
        product = nt(turned_ref[...], seq_ref[begin : begin + 256, :])
        live = (iota((1, 256), 1) + begin) < length
        qkv_ref[:, begin : begin + 256] = jnp.where(live, (product + bias) * scale, 0.0).astype(BF)

    table = segments(slots, length)
    counts = jnp.sum(table, axis=1, keepdims=True)
    table_low = table.astype(BF)
    live = iota((1, slots), 1) < length

    def gather_head(head, carry):
        q = qkv_ref[pl.ds(pl.multiple_of(head * HEAD_DIM, HEAD_DIM), HEAD_DIM), :]
        k = qkv_ref[pl.ds(pl.multiple_of(width + head * HEAD_DIM, HEAD_DIM), HEAD_DIM), :]
        v = qkv_ref[pl.ds(pl.multiple_of(2 * width + head * HEAD_DIM, HEAD_DIM), HEAD_DIM), :]
        land_query = nt(table_low, q) / counts
        land_keys = nt(table_low, k) / counts
        land_ref[0, head] = land_query
        land_ref[1, head] = land_keys
        scores = nn(land_query.astype(BF), k)
        weights = softmax_rows(jnp.where(live, scores, masked_score))
        land_ref[2, head] = nt(weights.astype(BF), v)
        return carry

    lax.fori_loop(0, heads, gather_head, 0)

    every = range(heads)
    eye = (iota((LAND, LAND), 0) == iota((LAND, LAND), 1)).astype(F32)
    kernels = [softmax_rows(nt(land_ref[0, h], land_ref[1, h], precision=highest)) for h in every]
    starts = []
    for h in every:
        land_ref[4, h] = kernels[h]
        column_top = jnp.max(jnp.sum(kernels[h], axis=0, keepdims=True), axis=1, keepdims=True)
        row_top = jnp.max(jnp.sum(kernels[h], axis=1, keepdims=True), axis=0, keepdims=True)
        starts.append(kernels[h].T / (column_top * row_top))

    def refine(step, approx):
        product = [nn(kernels[h], approx[h], precision=highest) for h in every]
        second = [15.0 * eye - nn(product[h], 7.0 * eye - product[h], precision=highest) for h in every]
        third = [13.0 * eye - nn(product[h], second[h], precision=highest) for h in every]
        for h in every:
            state_ref[step, 0, h] = approx[h]
            state_ref[step, 1, h] = product[h]
            state_ref[step, 2, h] = second[h]
            state_ref[step, 3, h] = third[h]
        return [0.25 * nn(approx[h], third[h], precision=highest) for h in every]

    inverse = lax.fori_loop(0, ITERS, refine, starts)
    for h in every:
        land_ref[3, h] = inverse[h]
        land_ref[5, h] = nn(inverse[h], land_ref[2, h], precision=highest)

    def mix_head(head, carry):
        q = qkv_ref[pl.ds(pl.multiple_of(head * HEAD_DIM, HEAD_DIM), HEAD_DIM), :]
        v = qkv_ref[pl.ds(pl.multiple_of(2 * width + head * HEAD_DIM, HEAD_DIM), HEAD_DIM), :]
        weights = softmax_columns(nn(land_ref[1, head].astype(BF), q))
        turned = land_ref[5, head].T.astype(BF)
        total = nn(turned, weights.astype(BF)) + conv_band(v, band_ref, head)
        mixed_ref[pl.ds(pl.multiple_of(head * HEAD_DIM, HEAD_DIM), HEAD_DIM), :] = total.astype(BF)
        return carry

    lax.fori_loop(0, heads, mix_head, 0)
    for key in range(count_ctx):
        spot = pl.multiple_of(jnp.bitwise_xor(own_ctx, key) * rows, rows)
        blocks_ref[key] = mixed_ref[:, pl.ds(spot, rows)]


def attend(scalars, tokens, weights, bands, heads, rows, shard):
    count_ctx, count_fsdp = len(tokens), len(weights)
    width = heads * HEAD_DIM
    slots = rows * count_ctx
    outs = (
        shape((slots, D), BF),
        shape((3 * width, D), BF),
        shape((3 * width, slots), BF),
        shape((count_fsdp * 8, 3 * width), BF),
        shape((6, heads, LAND, LAND), F32),
        shape((ITERS, 4, heads, LAND, LAND), F32),
        shape((count_ctx, width, rows), BF),
    )

    def body(*refs):
        attend_kernel((heads, rows, shard), count_ctx, count_fsdp, *refs)

    return pl.pallas_call(
        body,
        out_shape=outs,
        in_specs=[SMEM] + [ANY] * (count_ctx + count_fsdp) + [VMEM],
        out_specs=[VMEM] * len(outs),
        scratch_shapes=[
            pltpu.VMEM((D, 3 * width), BF),
            pltpu.VMEM((count_fsdp * 8, 3 * width), BF),
            pltpu.VMEM((width, slots), BF),
            pltpu.SemaphoreType.DMA((count_ctx + 2 * count_fsdp,)),
        ],
        cost_estimate=pl.CostEstimate(
            flops=4 * slots * D * 3 * width, bytes_accessed=60_000_000, transcendentals=0
        ),
        name="attend",
    )(scalars, *tokens, *weights, bands)


def attend_back_kernel(parts, count_ctx, count_fsdp, *refs):
    heads, rows, shard = parts
    width = heads * HEAD_DIM
    refs = list(refs)
    scalar_ref = refs.pop(0)
    grad_refs = [refs.pop(0) for _ in range(count_ctx)]
    (
        seq_ref,
        turned_ref,
        qkv_ref,
        land_ref,
        state_ref,
        band_ref,
        share_ref,
        keep_ref,
        send_ref,
        grad_ref,
        deep_ref,
        back_ref,
        taps_ref,
        copy_sem,
    ) = refs
    own_ctx = scalar_ref[0]
    length = scalar_ref[2]
    slots = rows * count_ctx
    copies = []
    for key in range(count_ctx):
        spot = pl.multiple_of(jnp.bitwise_xor(own_ctx, key) * rows, rows)
        copies.append(
            pltpu.make_async_copy(
                grad_refs[key], grad_ref.at[:, pl.ds(spot, rows)], copy_sem.at[key]
            )
        )
    fetch(copies)
    table = segments(slots, length)
    counts = jnp.sum(table, axis=1, keepdims=True)
    table_low = table.astype(BF)
    live = iota((1, slots), 1) < length
    every = range(heads)

    def rows_of(base, head):
        return pl.ds(pl.multiple_of(base + head * HEAD_DIM, HEAD_DIM), HEAD_DIM)

    def first(head, carry):
        q = qkv_ref[rows_of(0, head), :]
        g = grad_ref[rows_of(0, head), :]
        keys_low = land_ref[1, head].astype(BF)
        weights = softmax_columns(nn(keys_low, q))
        grad_mixing = nt(weights.astype(BF), g)
        slope = nn(land_ref[5, head].astype(BF), g)
        slope = (weights * (slope - jnp.sum(weights * slope, axis=0, keepdims=True))).astype(BF)
        deep_ref[1, head] = grad_mixing
        deep_ref[3, head] = nt(slope, q)
        back_ref[rows_of(0, head), :] = tn(keys_low, slope)
        return carry

    lax.fori_loop(0, heads, first, 0)
    for h in every:
        deep_ref[0, h] = nt(deep_ref[1, h], land_ref[2, h], precision=highest)
        deep_ref[1, h] = tn(land_ref[3, h], deep_ref[1, h], precision=highest)

    kernels = [land_ref[4, h] for h in every]
    eye = (iota((LAND, LAND), 0) == iota((LAND, LAND), 1)).astype(F32)

    def unwind(turn, carry):
        d_next, d_kernel = carry
        step = ITERS - 1 - turn
        approx = [state_ref[step, 0, h] for h in every]
        product = [state_ref[step, 1, h] for h in every]
        second = [state_ref[step, 2, h] for h in every]
        third = [state_ref[step, 3, h] for h in every]
        d_third = [0.25 * tn(approx[h], d_next[h], precision=highest) for h in every]
        d_approx = [0.25 * nt(d_next[h], third[h], precision=highest) for h in every]
        d_second = [-tn(product[h], d_third[h], precision=highest) for h in every]
        d_product = [-nt(d_third[h], second[h], precision=highest) for h in every]
        d_first = [-tn(product[h], d_second[h], precision=highest) for h in every]
        d_product = [
            d_product[h] - nt(d_second[h], 7.0 * eye - product[h], precision=highest) - d_first[h]
            for h in every
        ]
        d_kernel = [d_kernel[h] + nt(d_product[h], approx[h], precision=highest) for h in every]
        d_approx = [d_approx[h] + tn(kernels[h], d_product[h], precision=highest) for h in every]
        return d_approx, d_kernel

    d_start, d_kernel = lax.fori_loop(
        0,
        ITERS,
        unwind,
        ([deep_ref[0, h] for h in every], [jnp.zeros((LAND, LAND), F32) for _ in every]),
    )
    for h in every:
        kernel = kernels[h]
        column_sums = jnp.sum(kernel, axis=0, keepdims=True)
        row_sums = jnp.sum(kernel, axis=1, keepdims=True)
        column_top = jnp.max(column_sums, axis=1, keepdims=True)
        row_top = jnp.max(row_sums, axis=0, keepdims=True)
        scale = column_top * row_top
        turned = d_start[h].T
        d_scale = -jnp.sum(
            jnp.sum(turned * kernel, axis=1, keepdims=True), axis=0, keepdims=True
        ) / (scale * scale)
        column_hit = (column_sums == column_top).astype(F32)
        row_hit = (row_sums == row_top).astype(F32)
        column_hit = column_hit / jnp.sum(column_hit, axis=1, keepdims=True)
        row_hit = row_hit / jnp.sum(row_hit, axis=0, keepdims=True)
        slope = d_kernel[h] + turned / scale
        slope = slope + d_scale * row_top * column_hit + d_scale * column_top * row_hit
        slope = kernel * (slope - jnp.sum(kernel * slope, axis=1, keepdims=True))
        deep_ref[2, h] = nn(slope, land_ref[1, h], precision=highest)
        deep_ref[3, h] = deep_ref[3, h] + tn(slope, land_ref[0, h], precision=highest)

    table_twice = jnp.concatenate([table_low, table_low], axis=0)
    place, other = iota((TAPS_OUT, TAPS_OUT), 0), iota((TAPS_OUT, TAPS_OUT), 1)
    flip = (place + other == TAPS_OUT - 1).astype(BF)

    def second_pass(head, carry):
        k = qkv_ref[rows_of(width, head), :]
        v = qkv_ref[rows_of(2 * width, head), :]
        g = grad_ref[rows_of(0, head), :]
        query_low = land_ref[0, head].astype(BF)
        scores = nn(query_low, k)
        weights = softmax_rows(jnp.where(live, scores, masked_score))
        d_context = deep_ref[1, head].astype(BF)
        slope = nn(d_context, v)
        slope = (weights * (slope - jnp.sum(weights * slope, axis=1, keepdims=True))).astype(BF)
        d_query = (deep_ref[2, head] + nt(slope, k)) / counts
        d_keys = deep_ref[3, head] / counts
        high, low = halves(d_query)
        spread = tn(jnp.concatenate([high, low], axis=0), table_twice)
        d_q = (back_ref[rows_of(0, head), :] + spread).astype(BF)
        high, low = halves(d_keys)
        spread = tn(jnp.concatenate([high, low], axis=0), table_twice)
        d_k = (tn(query_low, slope) + spread).astype(BF)
        d_v = (tn(d_context, weights.astype(BF)) + conv_band(g, band_ref, head)).astype(BF)
        zero = jnp.zeros_like(d_q)
        back_ref[rows_of(0, head), :] = jnp.where(live, d_q.astype(F32) * 0.125, 0.0)
        back_ref[rows_of(width, head), :] = jnp.where(live, d_k.astype(F32), 0.0)
        back_ref[rows_of(2 * width, head), :] = jnp.where(live, d_v.astype(F32), 0.0)
        blocks = slots // TAPS_OUT
        edge = jnp.zeros((HEAD_DIM, TAPS_OUT), BF)
        padded = jnp.concatenate([edge, v, edge], axis=1)
        windows = jnp.concatenate(
            [padded[:, TAPS_OUT * b : TAPS_OUT * b + TAPS_IN] for b in range(blocks)], axis=0
        )
        places = jnp.concatenate(
            [g[:, TAPS_OUT * b : TAPS_OUT * (b + 1)] for b in range(blocks)], axis=0
        )
        flipped = nn(places, flip).astype(BF)
        square = tn(flipped, windows)
        slanted = pltpu.roll(square, TAPS_IN - 111 - TAPS_OUT, 1, stride=1, stride_axis=0)
        line = jnp.sum(slanted, axis=0, keepdims=True)
        taps_ref[pl.ds(pl.multiple_of(head * 8, 8), 8), :] = jnp.broadcast_to(
            line[:, :128], (8, 128)
        )
        return carry

    lax.fori_loop(0, heads, second_pass, 0)

    back_low = back_ref[...].astype(BF)
    entry = iota((width, 1), 0)
    spot = own_ctx * width + entry
    owner = jnp.floor((spot.astype(F32) + 0.5) * (1.0 / shard)).astype(jnp.int32)
    lane = spot - owner * shard
    pick_owner = ((iota((width, count_fsdp), 1) == owner) & (spot < D)).astype(F32)
    lines = []
    for base in (0, 2 * width):
        total = jnp.sum(back_ref[base : base + width, :], axis=1, keepdims=True)
        placed = jnp.where(iota((width, 128), 1) == lane, total, 0.0)
        lines.append(tn(pick_owner, placed, precision=highest))
    taps = jnp.concatenate(
        [taps_ref[8 * h : 8 * h + 1, :] for h in every]
        + [jnp.zeros((6 - heads, 128), F32)],
        axis=0,
    )
    taps = jnp.where(iota((6, 128), 1) < KSIZE, taps, 0.0)
    filler = jnp.zeros((8, 3 * width - 128), F32)
    grads = nn(back_low, seq_ref[...]).astype(BF).T
    for owner_index in range(count_fsdp):
        rest = jnp.concatenate(
            [lines[0][owner_index : owner_index + 1], lines[1][owner_index : owner_index + 1], taps],
            axis=0,
        )
        share_ref[owner_index, :shard] = grads[owner_index * shard : (owner_index + 1) * shard]
        share_ref[owner_index, shard:] = jnp.concatenate([rest, filler], axis=1).astype(BF)
    for key in range(count_ctx):
        spot = pl.multiple_of(jnp.bitwise_xor(own_ctx, key) * rows, rows)
        block = back_ref[:, pl.ds(spot, rows)].astype(BF)
        product = tn(block, turned_ref[...])
        if key % 2 == 0:
            keep_ref[key // 2] = product
        else:
            send_ref[key // 2] = product


def attend_back(scalars, grads, saved, bands, heads, rows, shard, count_fsdp):
    count_ctx = len(grads)
    width = heads * HEAD_DIM
    slots = rows * count_ctx
    sequence, turned, qkv, land, state = saved
    outs = (
        shape((count_fsdp, shard + 8, 3 * width), BF),
        shape((count_ctx // 2, rows, D), F32),
        shape((count_ctx // 2, rows, D), F32),
    )

    def body(*refs):
        attend_back_kernel((heads, rows, shard), count_ctx, count_fsdp, *refs)

    return pl.pallas_call(
        body,
        out_shape=outs,
        in_specs=[SMEM] + [ANY] * count_ctx + [VMEM] * 6,
        out_specs=[VMEM] * len(outs),
        scratch_shapes=[
            pltpu.VMEM((width, slots), BF),
            pltpu.VMEM((4, heads, LAND, LAND), F32),
            pltpu.VMEM((3 * width, slots), F32),
            pltpu.VMEM((8 * heads, 128), F32),
            pltpu.SemaphoreType.DMA((count_ctx,)),
        ],
        cost_estimate=pl.CostEstimate(
            flops=8 * slots * D * 3 * width, bytes_accessed=100_000_000, transcendentals=0
        ),
        name="attend_back",
    )(scalars, *grads, sequence, turned, qkv, land, state, bands)


def project_kernel(parts, count_ctx, count_fsdp, column, *refs):
    width, rows, shard = parts
    refs = list(refs)
    scalar_ref = refs.pop(0)
    mixed_refs = [refs.pop(0) for _ in range(count_ctx)]
    weight_refs = [refs.pop(0) for _ in range(count_fsdp)]
    (
        token_ref,
        small_ref,
        mixed_ref,
        out_ref,
        hidden_ref,
        low_ref,
        unit_ref,
        rate_ref,
        copy_sem,
    ) = refs
    own_ctx = scalar_ref[0]
    own_fsdp = scalar_ref[1]
    copies = []
    for key in range(count_ctx):
        spot = pl.multiple_of(jnp.bitwise_xor(own_ctx, key) * width, 8)
        copies.append(
            pltpu.make_async_copy(
                mixed_refs[key], mixed_ref.at[pl.ds(spot, width), :], copy_sem.at[len(copies)]
            )
        )
    for key in range(count_fsdp):
        spot = pl.multiple_of(jnp.bitwise_xor(own_fsdp, key) * shard, 8)
        copies.append(
            pltpu.make_async_copy(
                weight_refs[key].at[:, pl.ds(column, D)],
                out_ref.at[pl.ds(spot, shard), :],
                copy_sem.at[len(copies)],
            )
        )
    fetch(copies)
    mixer = tn(mixed_ref[:D, :], out_ref[...]) + small_ref[2:3, :]
    hidden_ref[...] = token_ref[...].astype(F32) + mixer

    def norm(step, carry):
        place = pl.ds(pl.multiple_of(step * 64, 64), 64)
        value = hidden_ref[place, :]
        average = jnp.mean(value, axis=-1, keepdims=True)
        centered = value - average
        rate = lax.rsqrt(jnp.mean(centered * centered, axis=-1, keepdims=True) + norm_eps)
        unit = centered * rate
        hidden = unit * small_ref[4:5, :] + small_ref[5:6, :]
        unit_ref[place, :] = unit
        rate_ref[place, :] = jnp.broadcast_to(rate, (64, 128))
        hidden_ref[place, :] = hidden
        low_ref[place, :] = hidden.astype(BF)
        return carry

    lax.fori_loop(0, rows // 64, norm, 0)


def project(scalars, mixed, weights, tokens, small, width, shard, column):
    count_ctx, count_fsdp = len(mixed), len(weights)
    rows = tokens.shape[0]
    outs = (
        shape((width * count_ctx, rows), BF),
        shape((D, D), BF),
        shape((rows, D), F32),
        shape((rows, D), BF),
        shape((rows, D), F32),
        shape((rows, 128), F32),
    )

    def body(*refs):
        project_kernel((width, rows, shard), count_ctx, count_fsdp, column, *refs)

    return pl.pallas_call(
        body,
        out_shape=outs,
        in_specs=[SMEM] + [ANY] * (count_ctx + count_fsdp) + [VMEM] * 2,
        out_specs=[VMEM] * len(outs),
        scratch_shapes=[pltpu.SemaphoreType.DMA((count_ctx + count_fsdp,))],
        cost_estimate=pl.CostEstimate(
            flops=2 * rows * D * D, bytes_accessed=12_000_000, transcendentals=0
        ),
        name="project",
    )(scalars, *mixed, *weights, tokens, small)


def lift_kernel(parts, count_fsdp, *refs):
    rows, shard, share = parts
    refs = list(refs)
    scalar_ref = refs.pop(0)
    own_ref = refs.pop(0)
    other_ref = refs.pop(0)
    up_refs = [refs.pop(0) for _ in range(count_fsdp)]
    down_refs = [refs.pop(0) for _ in range(count_fsdp)]
    (
        bias_ref,
        both_ref,
        up_ref,
        down_ref,
        active_ref,
        slope_ref,
        feed_ref,
        copy_sem,
    ) = refs
    own_fsdp = scalar_ref[1]
    copies = []
    for key in range(count_fsdp):
        owner = jnp.bitwise_xor(own_fsdp, key)
        spot = pl.multiple_of(owner * shard, 8)
        copies.append(
            pltpu.make_async_copy(
                up_refs[key].at[:, pl.ds(0, FF // 2)],
                up_ref.at[pl.ds(spot, shard), :],
                copy_sem.at[len(copies)],
            )
        )
        spot = pl.multiple_of(owner * share, 8)
        copies.append(
            pltpu.make_async_copy(
                down_refs[key], down_ref.at[pl.ds(spot, share), :], copy_sem.at[len(copies)]
            )
        )
    for copy in copies:
        copy.start()
    both_ref[:rows, :] = own_ref[...]
    both_ref[rows:, :] = other_ref[...]
    for copy in copies:
        copy.wait()

    def step(index, carry):
        place = pl.ds(pl.multiple_of(index * 128, 128), 128)
        lifted = nn(both_ref[place, :], up_ref[...]) + bias_ref[0:1, :]
        cdf = 0.5 * (1.0 + lax.erf(lifted * 0.7071067811865476))
        active = (lifted * cdf).astype(BF)
        active_ref[place, :] = active
        slope_ref[place, :] = cdf + lifted * (
            jnp.exp(-0.5 * lifted * lifted) * 0.3989422804014327
        )
        feed_ref[place, :] = nn(active, down_ref[...])
        return carry

    lax.fori_loop(0, 2 * rows // 128, step, 0)


def lift(scalars, own, other, ups, downs, bias, shard, share):
    count_fsdp = len(ups)
    rows = own.shape[0]
    outs = (
        shape((2 * rows, D), BF),
        shape((D, FF // 2), BF),
        shape((FF // 2, D), BF),
        shape((2 * rows, FF // 2), BF),
        shape((2 * rows, FF // 2), F32),
        shape((2 * rows, D), F32),
    )

    def body(*refs):
        lift_kernel((rows, shard, share), count_fsdp, *refs)

    return pl.pallas_call(
        body,
        out_shape=outs,
        in_specs=[SMEM, VMEM, VMEM] + [ANY] * (2 * count_fsdp) + [VMEM],
        out_specs=[VMEM] * len(outs),
        scratch_shapes=[pltpu.SemaphoreType.DMA((2 * count_fsdp,))],
        cost_estimate=pl.CostEstimate(
            flops=8 * rows * D * FF, bytes_accessed=40_000_000, transcendentals=0
        ),
        name="lift",
    )(scalars, own, other, *ups, *downs, bias)


def finish_kernel(
    scalar_ref,
    hidden_ref,
    own_ref,
    other_ref,
    small_ref,
    grad_ref,
    output_ref,
    second_ref,
    feed_ref,
    sums_ref,
):
    rows = hidden_ref.shape[0]
    begin = scalar_ref[0] * rows
    length = scalar_ref[2]

    def step(index, carry):
        gain_sum, shift_sum, feed_sum = carry
        place = pl.ds(pl.multiple_of(index * 64, 64), 64)
        value = hidden_ref[place, :] + (own_ref[place, :] + other_ref[place, :] + small_ref[3:4, :])
        average = jnp.mean(value, axis=-1, keepdims=True)
        centered = value - average
        rate = lax.rsqrt(jnp.mean(centered * centered, axis=-1, keepdims=True) + norm_eps)
        unit = centered * rate
        live = (iota((64, 1), 0) + begin + index * 64) < length
        normed = unit * small_ref[6:7, :] + small_ref[7:8, :]
        output_ref[place, :] = jnp.where(live, normed, 0.0).astype(BF)
        upstream = jnp.where(live, grad_ref[place, :].astype(F32), 0.0)
        scaled = upstream * small_ref[6:7, :]
        second = rate * (
            scaled
            - jnp.mean(scaled, axis=-1, keepdims=True)
            - unit * jnp.mean(scaled * unit, axis=-1, keepdims=True)
        )
        second_ref[place, :] = second
        low = second.astype(BF)
        feed_ref[place, :] = low

        def fold(block):
            return jnp.sum(block.reshape(8, 8, D), axis=0)

        return (
            gain_sum + fold(upstream * unit),
            shift_sum + fold(upstream),
            feed_sum + fold(low.astype(F32)),
        )

    zero = jnp.zeros((8, D), F32)
    totals = lax.fori_loop(0, rows // 64, step, (zero, zero, zero))
    sums_ref[...] = jnp.concatenate(
        [jnp.sum(total, axis=0, keepdims=True) for total in totals] + [jnp.zeros((5, D), F32)],
        axis=0,
    )


def finish(scalars, hidden, own, other, small, grads):
    rows = hidden.shape[0]
    outs = (
        shape((rows, D), BF),
        shape((rows, D), F32),
        shape((rows, D), BF),
        shape((8, D), F32),
    )
    return pl.pallas_call(
        finish_kernel,
        out_shape=outs,
        in_specs=[SMEM] + [VMEM] * 5,
        out_specs=[VMEM] * 4,
        cost_estimate=pl.CostEstimate(
            flops=30 * rows * D, bytes_accessed=9_000_000, transcendentals=0
        ),
        name="finish",
    )(scalars, hidden, own, other, small, grads)


def lower_kernel(
    own_ref, other_ref, slope_ref, up_ref, down_ref, both_ref, lifted_ref, hidden_ref, bias_ref
):
    rows = own_ref.shape[0]
    both_ref[:rows, :] = own_ref[...]
    both_ref[rows:, :] = other_ref[...]

    def step(index, total):
        place = pl.ds(pl.multiple_of(index * 128, 128), 128)
        slope = nt(both_ref[place, :], down_ref[...]) * slope_ref[place, :]
        low = slope.astype(BF)
        lifted_ref[place, :] = low
        hidden_ref[place, :] = nt(low, up_ref[...])
        return total + jnp.sum(low.astype(F32).reshape(16, 8, FF // 2), axis=0)

    total = lax.fori_loop(0, 2 * rows // 128, step, jnp.zeros((8, FF // 2), F32))
    bias_ref[...] = jnp.broadcast_to(jnp.sum(total, axis=0, keepdims=True), (8, FF // 2))


def lower(own, other, slope, up, down):
    rows = own.shape[0]
    outs = (
        shape((2 * rows, D), BF),
        shape((2 * rows, FF // 2), BF),
        shape((2 * rows, D), F32),
        shape((8, FF // 2), F32),
    )
    return pl.pallas_call(
        lower_kernel,
        out_shape=outs,
        in_specs=[VMEM] * 5,
        out_specs=[VMEM] * 4,
        cost_estimate=pl.CostEstimate(
            flops=8 * rows * D * FF, bytes_accessed=30_000_000, transcendentals=0
        ),
        name="lower",
    )(own, other, slope, up, down)


def unmix_kernel(
    parts,
    scalar_ref,
    second_ref,
    own_ref,
    other_ref,
    unit_ref,
    rate_ref,
    small_ref,
    weight_ref,
    first_ref,
    mixer_ref,
    blocks_ref,
    sums_ref,
    mixed_ref,
):
    width, count_ctx = parts
    rows = second_ref.shape[0]

    def step(index, carry):
        gain_sum, shift_sum, out_sum = carry
        place = pl.ds(pl.multiple_of(index * 64, 64), 64)
        upstream = (own_ref[place, :] + other_ref[place, :]) + second_ref[place, :]
        unit = unit_ref[place, :]
        scaled = upstream * small_ref[4:5, :]
        first = rate_ref[place, :1] * (
            scaled
            - jnp.mean(scaled, axis=-1, keepdims=True)
            - unit * jnp.mean(scaled * unit, axis=-1, keepdims=True)
        )
        first_ref[place, :] = first
        low = first.astype(BF)
        mixer_ref[place, :] = low

        def fold(block):
            return jnp.sum(block.reshape(8, 8, D), axis=0)

        return (
            gain_sum + fold(upstream * unit),
            shift_sum + fold(upstream),
            out_sum + fold(low.astype(F32)),
        )

    zero = jnp.zeros((8, D), F32)
    totals = lax.fori_loop(0, rows // 64, step, (zero, zero, zero))
    sums_ref[...] = jnp.concatenate(
        [jnp.sum(total, axis=0, keepdims=True) for total in totals] + [jnp.zeros((5, D), F32)],
        axis=0,
    )
    mixed_ref[:D, :] = nt(weight_ref[...], mixer_ref[...]).astype(BF)
    if mixed_ref.shape[0] > D:
        mixed_ref[D:, :] = jnp.zeros((mixed_ref.shape[0] - D, rows), BF)
    for key in range(count_ctx):
        spot = pl.multiple_of(jnp.bitwise_xor(scalar_ref[0], key) * width, HEAD_DIM)
        blocks_ref[key] = mixed_ref[pl.ds(spot, width), :]


def unmix(scalars, second, own, other, unit, rate, small, weight, width, count_ctx):
    rows = second.shape[0]
    outs = (
        shape((rows, D), F32),
        shape((rows, D), BF),
        shape((count_ctx, width, rows), BF),
        shape((8, D), F32),
    )

    def body(*refs):
        unmix_kernel((width, count_ctx), *refs)

    return pl.pallas_call(
        body,
        out_shape=outs,
        in_specs=[SMEM] + [VMEM] * 7,
        out_specs=[VMEM] * 4,
        scratch_shapes=[pltpu.VMEM((width * count_ctx, rows), BF)],
        cost_estimate=pl.CostEstimate(
            flops=2 * rows * D * D, bytes_accessed=12_000_000, transcendentals=0
        ),
        name="unmix",
    )(scalars, second, own, other, unit, rate, small, weight)


def spread_fsdp(piece):
    count = lax.axis_size("fsdp")
    pieces = [None] * count
    pieces[0] = piece
    for key in range(2, count, 2):
        pieces[key] = swap(piece, "fsdp", key)
    for key in range(0, count, 2):
        pieces[key + 1] = swap(pieces[key], "fsdp", 1)
    return pieces


def tree_sum(terms):
    while len(terms) > 1:
        terms = [terms[i] + terms[i + 1] for i in range(0, len(terms), 2)]
    return terms[0]


def pick(block, index, axis):
    return lax.dynamic_index_in_dim(block, index, axis, keepdims=False)


def gather_back(share, axis, index, keys):
    pieces = {0: share}
    for key in keys:
        pieces[key] = swap(share, axis, key)
    return pieces


def reduce_fsdp(block):
    count = block.shape[0]
    own = lax.axis_index("fsdp")
    rest = block.shape[1:]
    pairs = block.reshape((count // 2, 2) + rest)
    kept = pick(pairs, own % 2, 1)
    came = swap(pick(pairs, 1 - own % 2, 1), "fsdp", 1)
    column = (kept.astype(F32) + came.astype(F32)).astype(BF)
    place = own // 2
    terms = [pick(column, place, 0).astype(F32)]
    for key in range(1, count // 2):
        terms.append(swap(pick(column, place ^ key, 0), "fsdp", 2 * key).astype(F32))
    return tree_sum(terms)


def reduce_rows(block):
    count, rows, columns = block.shape
    chips = lax.axis_size("ctx") // 2
    place = lax.axis_index("ctx") // 2
    parts = block.reshape(count, chips, rows // chips, columns)
    terms = [pick(parts, place, 1).astype(F32)]
    for key in range(1, chips):
        terms.append(swap(pick(parts, place ^ key, 1), "ctx", 2 * key).astype(F32))
    total = reduce_fsdp(tree_sum(terms).astype(BF)).astype(BF)
    pieces = [total]
    for key in range(1, chips):
        pieces.append(swap(total, "ctx", 2 * key))
    stacked = jnp.stack(pieces)
    ordered = stacked[jnp.arange(chips) ^ place] if chips > 2 else by_bit(stacked, place)
    return ordered.reshape(rows, columns)


def by_bit(stacked, bit):
    return jnp.where(bit == 0, stacked, stacked[::-1])


def per_device(
    tokens,
    cotangent,
    lengths,
    w_query,
    w_key,
    w_value,
    w_out,
    w_up,
    w_down,
    b_query,
    b_value,
    b_out,
    b_up,
    b_down,
    gain_first,
    shift_first,
    gain_second,
    shift_second,
    conv_taps,
):
    own_tokens = tokens[0]
    rows = own_tokens.shape[0]
    count_ctx = lax.axis_size("ctx")
    count_fsdp = lax.axis_size("fsdp")
    own_ctx = lax.axis_index("ctx")
    own_fsdp = lax.axis_index("fsdp")
    core = own_ctx % 2
    length = lengths[0]
    heads = -(-HEADS // count_ctx)
    width = heads * HEAD_DIM
    shard = w_query.shape[0]
    share = w_down.shape[0] // 2
    scalars = jnp.stack([own_ctx, own_fsdp, length, length]).astype(jnp.int32)

    token_pieces = [own_tokens]
    for key in range(2, count_ctx, 2):
        token_pieces += [None, swap(own_tokens, "ctx", key)]
    token_pieces.append(None)
    for key in range(0, count_ctx, 2):
        token_pieces[key + 1] = swap(token_pieces[key], "ctx", 1)

    def own_columns(weight):
        weight = jnp.pad(weight, ((0, 0), (0, width * count_ctx - D)))
        return lax.dynamic_slice_in_dim(weight, own_ctx * width, width, 1)

    vectors = jnp.stack(
        [b_query, b_value, b_out, b_down, gain_first, shift_first, gain_second, shift_second]
    )
    vectors = jnp.concatenate(
        [
            jnp.pad(vectors, ((0, 0), (0, 128 - shard))),
            jnp.pad(b_up[None, :], ((0, 7), (0, 3 * width - 128 - b_up.shape[0]))),
        ],
        axis=1,
    )
    qkv_piece = jnp.concatenate(
        [
            jnp.concatenate([own_columns(w) for w in (w_query, w_key, w_value)], axis=1),
            vectors,
        ],
        axis=0,
    ).astype(BF)
    qkv_pieces = spread_fsdp(qkv_piece)
    own_up = pick(w_up.reshape(shard, count_fsdp, 2, share), core, 2).reshape(shard, FF // 2)
    up_piece = jnp.concatenate([own_up, w_out], axis=1).astype(BF)
    down_piece = pick(w_down.reshape(2, share, D), core, 0).astype(BF)
    up_piece, down_piece, *_ = lax.optimization_barrier((up_piece, down_piece, *qkv_pieces))
    up_pieces = spread_fsdp(up_piece)
    down_pieces = spread_fsdp(down_piece)

    own_taps = lax.dynamic_slice_in_dim(
        jnp.pad(conv_taps, ((0, heads * count_ctx - HEADS), (0, 0))), own_ctx * heads, heads, 0
    )
    ahead, behind = taps_bands(own_taps)

    sequence, turned, qkv, small, land, state, blocks = attend(
        scalars, token_pieces, qkv_pieces, ahead, heads, rows, shard
    )
    small = small.reshape(count_fsdp, 8, 3 * width)
    vectors = small[:, :, :shard].transpose(1, 0, 2).reshape(8, D).astype(F32)
    up_bias = small[:, 0, 128 : 128 + 2 * share].reshape(count_fsdp, 2, share)
    up_bias = pick(up_bias, core, 1).reshape(1, FF // 2).astype(F32)
    up_bias = jnp.broadcast_to(up_bias, (8, FF // 2))

    mixed_pieces = [blocks[0]] + [swap(blocks[k], "ctx", k) for k in range(1, count_ctx)]
    mixed, out_weight, hidden, hidden_low, unit, rate = project(
        scalars, mixed_pieces, up_pieces, own_tokens, vectors, width, shard, FF // 2
    )
    hidden_other = swap(hidden_low, "ctx", 1)
    both, up_weight, down_weight, active, slope, feed = lift(
        scalars, hidden_low, hidden_other, up_pieces, down_pieces, up_bias, shard, share
    )
    feed_other = swap(feed[rows:], "ctx", 1)
    output, d_second, d_feed, second_sums = finish(
        scalars, hidden, feed[:rows], feed_other, vectors, cotangent[0]
    )
    d_feed_other = swap(d_feed, "ctx", 1)
    d_feed_both, d_lifted, d_hidden, d_up_bias = lower(
        d_feed, d_feed_other, slope, up_weight, down_weight
    )
    d_hidden_other = swap(d_hidden[rows:], "ctx", 1)
    grad_down = jnp.einsum("tf,td->fd", active, d_feed_both, preferred_element_type=F32).astype(BF)
    grad_up = jnp.einsum("td,tf->df", both, d_lifted, preferred_element_type=F32).astype(BF)
    d_first, d_mixer, d_blocks, first_sums = unmix(
        scalars,
        d_second,
        d_hidden[:rows],
        d_hidden_other,
        unit,
        rate,
        vectors,
        out_weight,
        width,
        count_ctx,
    )
    grad_out = jnp.dot(mixed[:D], d_mixer, preferred_element_type=F32).astype(BF)

    grad_pieces = [d_blocks[0]] + [swap(d_blocks[k], "ctx", k) for k in range(1, count_ctx)]
    qkv_share, near_keep, near_send = attend_back(
        scalars,
        grad_pieces,
        (sequence, turned, qkv, land, state),
        behind,
        heads,
        rows,
        shard,
        count_fsdp,
    )

    down_total = reduce_rows(grad_down.reshape(count_fsdp, share, D))
    out_halves = grad_out.reshape(count_fsdp, shard, 2, D // 2)
    out_half = pick(out_halves, core, 2).astype(F32) + swap(
        pick(out_halves, 1 - core, 2), "ctx", 1
    ).astype(F32)
    sums = jnp.concatenate([first_sums[:3], second_sums[:3]], axis=0)
    rest = jnp.concatenate(
        [
            jnp.pad(
                d_up_bias[0].reshape(count_fsdp, 1, share),
                ((0, 0), (0, 0), (0, FF // 2 + D // 2 - share)),
            ),
            jnp.pad(
                sums.reshape(6, count_fsdp, shard).transpose(1, 0, 2),
                ((0, 0), (0, 9), (0, FF // 2 + D // 2 - shard)),
            ),
        ],
        axis=1,
    ).astype(BF)
    up_block = jnp.concatenate(
        [grad_up.reshape(count_fsdp, shard, FF // 2), out_half.astype(BF)], axis=2
    )
    up_total = reduce_rows(jnp.concatenate([up_block, rest], axis=1))
    down_other = swap(down_total, "ctx", 1)
    up_other = swap(up_total, "ctx", 1)
    down_both = by_bit(jnp.stack([down_total, down_other]), core)
    up_both = by_bit(jnp.stack([up_total, up_other]), core)
    grad_w_down = down_both.reshape(2 * share, D).astype(F32)
    grad_w_up = (
        up_both[:, :shard, : FF // 2]
        .reshape(2, shard, count_fsdp, share)
        .transpose(1, 2, 0, 3)
        .reshape(shard, FF)
        .astype(F32)
    )
    grad_w_out = up_both[:, :shard, FF // 2 :].transpose(1, 0, 2).reshape(shard, D).astype(F32)
    grad_b_up = up_both[:, shard, :share].reshape(2 * share).astype(F32)
    small_sums = up_both[:, shard + 1 : shard + 7, :shard].astype(F32)
    small_sums = small_sums[0] + small_sums[1]

    qkv_total = reduce_fsdp(qkv_share).astype(BF)
    chips = count_ctx // 2
    totals = [qkv_total] + [swap(qkv_total, "ctx", 2 * key) for key in range(1, chips)]
    stacked = jnp.stack(totals)
    pairs = jnp.stack([stacked, swap(stacked, "ctx", 1)], axis=1)
    pairs = jnp.where(core == 0, pairs, pairs[:, ::-1])
    if chips == 2:
        pairs = by_bit(pairs, own_ctx // 2)
    else:
        pairs = pairs[jnp.arange(chips) ^ (own_ctx // 2)]
    pairs = pairs.reshape(count_ctx, shard + 8, 3 * width)

    def columns(begin):
        part = pairs[:, :shard, begin : begin + width].transpose(1, 0, 2)
        return part.reshape(shard, count_ctx * width)[:, :D].astype(F32)

    grad_w_query, grad_w_key, grad_w_value = columns(0), columns(width), columns(2 * width)
    grad_b_query = jnp.sum(pairs[:, shard, :shard].astype(F32), axis=0)
    grad_b_value = jnp.sum(pairs[:, shard + 1, :shard].astype(F32), axis=0)
    grad_taps = pairs[:, shard + 2 : shard + 2 + heads, :KSIZE].reshape(-1, KSIZE)[:HEADS].astype(F32)

    near = near_keep + swap(near_send, "ctx", 1)
    total = d_first + near[0]
    for key in range(1, chips):
        total = total + swap(near[key].astype(BF), "ctx", 2 * key).astype(F32)
    live = (own_ctx * rows + jnp.arange(rows, dtype=jnp.int32) < length)[:, None]
    input_grad = jnp.where(live, total, 0.0).astype(BF)

    return (
        output[None],
        input_grad[None],
        grad_w_query,
        grad_w_key,
        grad_w_value,
        grad_w_out,
        grad_w_up,
        grad_w_down,
        grad_b_query,
        grad_b_value,
        small_sums[2],
        grad_b_up,
        small_sums[5],
        small_sums[0],
        small_sums[1],
        small_sums[3],
        small_sums[4],
        grad_taps,
    )


def solution(mesh):
    vector = P("fsdp")
    matrix = P("fsdp", None)
    sequence = P("fsdp", "ctx", None)
    return jax.shard_map(
        per_device,
        mesh=mesh,
        in_specs=(sequence, sequence, vector) + (matrix,) * 6 + (vector,) * 9 + (P(),),
        out_specs=(sequence, sequence) + (matrix,) * 6 + (vector,) * 9 + (P(),),
        check_vma=False,
    )
```
